32 devices in a mesh: grp: 2 (over y), seq: 4 (over z), head: 2 (over x), dat: 2 (over core).
Axes of the slice: x: 2, y: 2, z: 4, core: 2. Of those that a mesh axis runs over, the one named last changes fastest.
Arguments:
- queries: bfloat16 [4, 256, 3072], P(('grp', 'dat'), 'seq', 'head'), parts along dimension 0, may hold values from -10 to 10
- keys: bfloat16 [4, 256, 512], P(('grp', 'dat'), 'seq', 'head'), parts along dimension 0, may hold values from -6 to 6
- values: bfloat16 [4, 256, 512], P(('grp', 'dat'), 'seq', 'head'), parts along dimension 0, may hold values from -6 to 6
- residual_in: bfloat16 [4, 256, 3072], P(('grp', 'dat'), 'seq', 'head'), parts along dimension 0, may hold values from -40 to 40
- out_proj: bfloat16 [24, 128, 3072], P('head', 'seq'), may hold values from -0.5 to 0.5
- norm_gain: bfloat16 [3072], replicated, may hold values from 0.5 to 1.5
- expert_gate: bfloat16 [4, 3072, 8192], P('head', None, 'seq'), may hold values from -0.109375 to 0.109375
- expert_up: bfloat16 [4, 3072, 8192], P('head', None, 'seq'), may hold values from -0.109375 to 0.109375
- routes: int32 [4, 256, 2], P(('grp', 'dat'), 'seq'), parts along dimension 0, may hold values from 0 to 3, as said below
- gate_numer: int32 [4, 256], P(('grp', 'dat'), 'seq'), parts along dimension 0, may hold values from 64 to 191
- sequence_lengths: int32 [4], P(('grp', 'dat')), parts along dimension 0, may hold values from 128 to 256, as said below
Outputs:
- stream: bfloat16 [4, 256, 3072], P(('grp', 'dat'), 'seq', 'head'), parts along dimension 0
- expert_hidden: bfloat16 [4, 4, 160, 8192], P('head', ('grp', 'dat'), None, 'seq'), parts along dimension 1
The draws below stay inside these ranges and needn't reach their ends.
There are 2 independent parts, one for each index of `grp`. The reference program is written for one: setup_inputs(seed, part) draws one part's arguments, and reference() takes and returns one part's arrays. A program takes and returns all parts, laid end to end along the dimension named above; an argument that names none is the same for every part. Nothing has to cross between parts.
Inputs may be any that keep to these rules, and one draw needn't show every extreme that they name: `routes`: for each sequence one expert is named by exactly 40 tokens of every aligned block of 64 positions, every other expert by at most 40 tokens of such a block; the two experts of a token differ. `sequence_lengths`: one sequence of the batch has the full length 256.
All inputs are finite; a program needn't handle non-finite values.
Results may differ from the reference program's by a relative error of at most 0.019.
Values may be sent and summed in bfloat16 or wider, within the bound.
A program may use at most 128 MiB of HBM per device.

```python
import math
import jax
import jax.numpy as jnp
from jax import lax

D = 3072
QUERY_HEAD_COUNT = 24
KEY_VALUE_HEADS = 4
HEAD_SIZE = 128
EXPERTS = 4
FF = 8192
TOK_DEV = 64
MOST = 40
SEQUENCE_LENGTH = 256
SLOTS = 160
BATCH_SEQUENCES = 2
N_SEQ = 4


def draw_queries(key, part):
    array_shape = (BATCH_SEQUENCES, SEQUENCE_LENGTH, QUERY_HEAD_COUNT * HEAD_SIZE)
    draws = jnp.clip(jax.random.normal(jax.random.fold_in(key, 11), array_shape, jnp.float32), -6.0, 6.0)
    return draws.astype(jnp.bfloat16)


def draw_keys(key, part):
    array_shape = (BATCH_SEQUENCES, SEQUENCE_LENGTH, KEY_VALUE_HEADS * HEAD_SIZE)
    draws = jnp.clip(jax.random.normal(jax.random.fold_in(key, 21), array_shape, jnp.float32), -6.0, 6.0)
    return draws.astype(jnp.bfloat16)


def draw_residual_in(key, part):
    array_shape = (BATCH_SEQUENCES, SEQUENCE_LENGTH, D)
    col_frac = jnp.arange(D, dtype=jnp.float32) / D
    row_scale = jnp.exp(jax.random.uniform(jax.random.fold_in(key, 31), (BATCH_SEQUENCES, SEQUENCE_LENGTH, 1), jnp.float32, math.log(0.3), math.log(3.0)))
    col_scale = 10.0 ** (col_frac - 0.7)
    noise_part = jnp.clip(jax.random.normal(jax.random.fold_in(key, 34), array_shape, jnp.float32), -6.0, 6.0)
    values = noise_part * col_scale * row_scale
    return values.astype(jnp.bfloat16)


def block_ranks(sub_key):
    return jax.random.permutation(sub_key, TOK_DEV)


def draw_routes(key, part):
    per_row = SEQUENCE_LENGTH // TOK_DEV
    blocks = BATCH_SEQUENCES * per_row
    others = EXPERTS - 1
    hot_expert = jnp.repeat(jax.random.randint(jax.random.fold_in(key, 41), (BATCH_SEQUENCES, 1), 0, EXPERTS), per_row, axis=0)
    rank_in_block = jax.vmap(block_ranks)(jax.random.split(jax.random.fold_in(key, 42), blocks)).astype(jnp.int32)
    turn_first = jax.random.randint(jax.random.fold_in(key, 43), (blocks, 1), 0, others)
    turn_second = jax.random.randint(jax.random.fold_in(key, 44), (blocks, 1), 0, others)
    in_hot = rank_in_block < MOST
    rest = rank_in_block - MOST
    partner = (hot_expert + 1 + (rank_in_block + turn_first) % others) % EXPERTS
    first_other = (hot_expert + 1 + (rest + turn_second) % others) % EXPERTS
    second_other = (hot_expert + 1 + (rest + turn_second + 1) % others) % EXPERTS
    first_pick = jnp.where(in_hot, hot_expert, first_other)
    second = jnp.where(in_hot, partner, second_other)
    flip_order = jax.random.randint(jax.random.fold_in(key, 45), (blocks, TOK_DEV), 0, 2) == 1
    lead = jnp.where(flip_order, second, first_pick)
    trail = jnp.where(flip_order, first_pick, second)
    return jnp.stack([lead, trail], axis=-1).reshape(BATCH_SEQUENCES, SEQUENCE_LENGTH, 2).astype(jnp.int32)


def draw_sequence_lengths(key, part):
    lengths_drawn = jax.random.randint(jax.random.fold_in(key, 51), (BATCH_SEQUENCES,), SEQUENCE_LENGTH // 2, SEQUENCE_LENGTH + 1)
    full_row = jax.random.randint(jax.random.fold_in(key, 52), (), 0, BATCH_SEQUENCES)
    return jnp.where(jnp.arange(BATCH_SEQUENCES) == full_row, SEQUENCE_LENGTH, lengths_drawn).astype(jnp.int32)


def plant(values, stream_key, least, high):
    shape = values.shape
    index_at = [jax.random.randint(jax.random.fold_in(stream_key, axis), (), 0, shape[axis]) for axis in range(len(shape))]
    values = values.at[tuple(index_at)].set(least)
    longest = shape.index(max(shape))
    index_at[longest] = (index_at[longest] + 1) % shape[longest]
    return values.at[tuple(index_at)].set(high)


def level_of(own_key, extent, cuts, least, largest):
    loudness, own = 1.0, jax.random.fold_in(own_key, 6)
    for dim, blocks in cuts:
        heights = jnp.exp(jax.random.uniform(jax.random.fold_in(own, dim), (blocks,), jnp.float32, least / len(cuts), largest / len(cuts)))
        loudness = loudness * jnp.repeat(heights, extent[dim] // blocks).reshape([-1 if axis == dim else 1 for axis in range(len(extent))])
    return loudness


def gaussian(key, extent, spread, most, pieces=(), kind=jnp.bfloat16):
    values = spread * jax.random.normal(key, extent, jnp.float32)
    if pieces:
        values = values * level_of(key, extent, pieces, -0.22, 0.18)
    return jnp.clip(values, -most, most).astype(kind)


def setup_inputs(seed: int = 0, part: int = 0) -> dict:
    splits = jax.random.split(jax.random.key(seed), 12)
    own_keys = jax.random.split(jax.random.fold_in(splits[11], part), 12)
    queries = draw_queries(jax.random.fold_in(jax.random.fold_in(splits[11], part), 71), part)
    keys = draw_keys(jax.random.fold_in(jax.random.fold_in(splits[11], part), 71), part)
    values = gaussian(own_keys[2], (BATCH_SEQUENCES, SEQUENCE_LENGTH, KEY_VALUE_HEADS * HEAD_SIZE), 1.0, 6.0, ((0, 2), (1, 4), (2, 2)))
    residual_in = draw_residual_in(jax.random.fold_in(jax.random.fold_in(splits[11], part), 71), part)
    out_proj = gaussian(splits[4], (QUERY_HEAD_COUNT, HEAD_SIZE, D), HEAD_SIZE ** -0.5, 0.5, ((0, 2), (1, 4)))
    norm_gain = jnp.clip(1.0 + 0.1 * jax.random.normal(splits[5], (D,), jnp.float32), 0.5, 1.5).astype(jnp.bfloat16)
    expert_gate = gaussian(splits[6], (EXPERTS, D, FF), D ** -0.5, 0.109375, ((0, 2), (2, 4)))
    expert_up = gaussian(splits[7], (EXPERTS, D, FF), D ** -0.5, 0.109375, ((0, 2), (2, 4)))
    routes = draw_routes(jax.random.fold_in(jax.random.fold_in(splits[11], part), 71), part)
    gate_numer = plant(jax.random.randint(own_keys[9], (BATCH_SEQUENCES, SEQUENCE_LENGTH), 64, 192), jax.random.fold_in(own_keys[9], 1), 64, 191).astype(jnp.int32)
    sequence_lengths = draw_sequence_lengths(jax.random.fold_in(jax.random.fold_in(splits[11], part), 71), part)
    return dict(queries=queries, keys=keys, values=values, residual_in=residual_in, out_proj=out_proj, norm_gain=norm_gain, expert_gate=expert_gate, expert_up=expert_up, routes=routes, gate_numer=gate_numer, sequence_lengths=sequence_lengths)


EPS = 1e-05
NEG = -1e+30

def slot_sources(marked, capacity):
    tok_len = marked.shape[1]
    counted = jnp.cumsum(marked, axis=1)
    rank_ids = jnp.arange(capacity, dtype=jnp.int32)
    source = lax.optimization_barrier(jnp.sum((counted[:, None, :] <= rank_ids[None, :, None]).astype(jnp.int32), axis=2))
    filled = rank_ids[None, :] < counted[:, -1:]
    source = jnp.minimum(source, tok_len - 1).astype(jnp.int32)
    return (source, filled)

def expert_rows(rows_in, slot_gate, gate_matrix, up_matrix):
    gate_part = jnp.dot(rows_in, gate_matrix, preferred_element_type=jnp.float32)
    up_part = jnp.dot(rows_in, up_matrix, preferred_element_type=jnp.float32)
    return (slot_gate[:, None] * (jax.nn.silu(gate_part) * up_part)).astype(jnp.bfloat16)

def reference(queries, keys, values, residual_in, out_proj, norm_gain, expert_gate, expert_up, routes, gate_numer, sequence_lengths):
    heads_per_group = QUERY_HEAD_COUNT // KEY_VALUE_HEADS
    score_scale = 1.0 / math.sqrt(HEAD_SIZE)
    positions = jnp.arange(SEQUENCE_LENGTH, dtype=jnp.int32)
    grouped_queries = queries.reshape(BATCH_SEQUENCES, SEQUENCE_LENGTH, KEY_VALUE_HEADS, heads_per_group, HEAD_SIZE).transpose(0, 2, 1, 3, 4).reshape(BATCH_SEQUENCES * KEY_VALUE_HEADS, SEQUENCE_LENGTH, heads_per_group, HEAD_SIZE)
    grouped_keys = keys.reshape(BATCH_SEQUENCES, SEQUENCE_LENGTH, KEY_VALUE_HEADS, HEAD_SIZE).transpose(0, 2, 1, 3).reshape(BATCH_SEQUENCES * KEY_VALUE_HEADS, SEQUENCE_LENGTH, HEAD_SIZE)
    grouped_values = values.reshape(BATCH_SEQUENCES, SEQUENCE_LENGTH, KEY_VALUE_HEADS, HEAD_SIZE).transpose(0, 2, 1, 3).reshape(BATCH_SEQUENCES * KEY_VALUE_HEADS, SEQUENCE_LENGTH, HEAD_SIZE)
    group_bounds = jnp.repeat(sequence_lengths, KEY_VALUE_HEADS)

    def attend(inputs):
        query_block, key_block, value_block, valid_len = inputs
        scores = jnp.einsum('thd,nd->htn', query_block.astype(jnp.float32), key_block.astype(jnp.float32), precision=lax.Precision.HIGHEST) * score_scale
        allowed = (positions[None, :] <= positions[:, None]) & (positions < valid_len)[None, :]
        scores = jnp.where(allowed[None], scores, NEG)
        top_score = lax.optimization_barrier(jnp.max(scores, axis=-1, keepdims=True))
        weights = jnp.where(allowed[None], jnp.exp(scores - top_score), 0.0)
        denom_sum = lax.optimization_barrier(jnp.sum(weights, axis=-1))
        rounded = lax.optimization_barrier(weights.astype(jnp.bfloat16)).astype(jnp.float32)
        weighted = jnp.einsum('htn,nd->thd', rounded, value_block.astype(jnp.float32), precision=lax.Precision.HIGHEST)
        return (weighted / denom_sum.T[:, :, None]).astype(jnp.bfloat16)
    attended_values = lax.map(attend, (grouped_queries, grouped_keys, grouped_values, group_bounds))
    attended_values = attended_values.reshape(BATCH_SEQUENCES, KEY_VALUE_HEADS, SEQUENCE_LENGTH, heads_per_group, HEAD_SIZE).transpose(0, 2, 1, 3, 4).reshape(BATCH_SEQUENCES * SEQUENCE_LENGTH, QUERY_HEAD_COUNT * HEAD_SIZE)
    mixed_sum = jnp.dot(attended_values, out_proj.reshape(QUERY_HEAD_COUNT * HEAD_SIZE, D), preferred_element_type=jnp.float32)
    stream = (residual_in.reshape(BATCH_SEQUENCES * SEQUENCE_LENGTH, D).astype(jnp.float32) + mixed_sum).astype(jnp.bfloat16)
    as_float = stream.astype(jnp.float32)
    mean_sq = lax.optimization_barrier(jnp.mean(as_float * as_float, axis=1, keepdims=True))
    normed = (as_float * lax.rsqrt(mean_sq + EPS) * norm_gain.astype(jnp.float32)).astype(jnp.bfloat16)
    first_weight = gate_numer.astype(jnp.float32) / 256.0
    blocks = BATCH_SEQUENCES * N_SEQ

    def one_expert(inputs):
        gate_matrix, up_matrix, expert_id = inputs
        gates = jnp.where(routes[..., 0] == expert_id, first_weight, 0.0) + jnp.where(routes[..., 1] == expert_id, 1.0 - first_weight, 0.0)
        marked = (gates > 0).astype(jnp.int32).reshape(blocks, TOK_DEV)
        source, filled = slot_sources(marked, MOST)
        flat_index = (jnp.arange(blocks, dtype=jnp.int32)[:, None] * TOK_DEV + source).reshape(-1)
        rows_in = jnp.take(normed, flat_index, axis=0)
        slot_gate = jnp.where(filled.reshape(-1), jnp.take(gates.reshape(-1), flat_index), 0.0)
        return expert_rows(rows_in, slot_gate, gate_matrix, up_matrix).reshape(BATCH_SEQUENCES, SLOTS, FF)
    hidden = lax.map(one_expert, (expert_gate, expert_up, jnp.arange(EXPERTS, dtype=jnp.int32)))
    return (stream.reshape(BATCH_SEQUENCES, SEQUENCE_LENGTH, D), hidden)
```

```python
import functools
import math

import jax
import jax.numpy as jnp
from jax import lax
from jax.experimental import pallas as pl
from jax.experimental.pallas import tpu as pltpu
from jax.sharding import PartitionSpec as P

HEAD_SIZE = 128
MOST = 40
EPS = 1e-05
NEG = -1e30
MESH = pl.DeviceIdType.MESH
F32 = jnp.float32
BF16 = jnp.bfloat16


def mix_kernel(
    n, m, nd,
    len_ref, q_ref, k_ref, v_ref, meta_ref, res_ref, w_ref,
    st_ref, own_ref, metas_ref,
    kbuf, vbuf, wbuf, cut, abuf, part, rbuf,
    k_s, k_r, v_s, v_r, me_s, me_r, w_s, w_r, wf_s, wf_r, wl,
    a_s, a_r, af_s, af_r, r_s, r_r, t_s, t_r, tx_s, tx_r,
):
    z = lax.axis_index("seq")
    x = lax.axis_index("head")
    c = lax.axis_index("dat")
    tok = q_ref.shape[0]
    heads = q_ref.shape[1] // HEAD_SIZE
    groups = k_ref.shape[1] // HEAD_SIZE
    per = heads // groups
    width = HEAD_SIZE // n
    share = res_ref.shape[1]
    wide = share // nd

    def peer(me, k, size):
        return lax.rem(me + k, size)

    def source(me, k, size):
        return lax.rem(me - k + size, size)

    sends = []

    def send(src, dst, s_sem, r_sem, where):
        copy = pltpu.make_async_remote_copy(
            src_ref=src, dst_ref=dst, send_sem=s_sem, recv_sem=r_sem,
            device_id=where, device_id_type=MESH,
        )
        copy.start()
        sends.append(copy)

    def arrived(dst, s_sem, r_sem, where):
        pltpu.make_async_remote_copy(
            src_ref=dst, dst_ref=dst, send_sem=s_sem, recv_sem=r_sem,
            device_id=where, device_id_type=MESH,
        ).wait_recv()

    barrier = pltpu.get_barrier_semaphore()
    for axis, me, size in (("seq", z, n), ("head", x, m), ("dat", c, nd)):
        for k in range(1, size):
            pl.semaphore_signal(barrier, inc=1, device_id={axis: peer(me, k, size)}, device_id_type=MESH)
    local_w = []
    for i in range(nd):
        start = pl.multiple_of(x * share + i * wide, 128)
        local = pltpu.make_async_copy(w_ref.at[:, pl.ds(start, wide)], wbuf.at[x, i], wl.at[i])
        local.start()
        local_w.append(local)
    pl.semaphore_wait(barrier, n - 1 + m - 1 + nd - 1)

    for k in range(1, n):
        to = {"seq": peer(z, k, n)}
        send(k_ref, kbuf.at[z], k_s.at[k - 1], k_r.at[k - 1], to)
        send(v_ref, vbuf.at[z], v_s.at[k - 1], v_r.at[k - 1], to)
    for j in range(1, m):
        to = peer(x, j, m)
        start = pl.multiple_of(to * share + c * wide, 128)
        send(w_ref.at[:, pl.ds(start, wide)], wbuf.at[x, c], w_s.at[j - 1], w_r.at[j - 1], {"head": to})
    for k in range(1, n):
        send(meta_ref, metas_ref.at[z], me_s.at[k - 1], me_r.at[k - 1], {"seq": peer(z, k, n)})
    kbuf[z] = k_ref[...]
    vbuf[z] = v_ref[...]
    metas_ref[z] = meta_ref[...]

    for k in range(1, n):
        s = source(z, k, n)
        arrived(kbuf.at[s], k_s.at[k - 1], k_r.at[k - 1], {"seq": s})
        arrived(vbuf.at[s], v_s.at[k - 1], v_r.at[k - 1], {"seq": s})

    row = lax.broadcasted_iota(jnp.int32, (per * tok, n * tok), 0)
    col = lax.broadcasted_iota(jnp.int32, (per * tok, n * tok), 1)
    allowed = (col <= lax.rem(row, tok) + z * tok) & (col < len_ref[0])
    scale = 1.0 / math.sqrt(HEAD_SIZE)
    done = []
    for g in range(groups):
        lanes = slice(g * HEAD_SIZE, (g + 1) * HEAD_SIZE)
        queries = jnp.concatenate(
            [q_ref[:, (g * per + i) * HEAD_SIZE : (g * per + i + 1) * HEAD_SIZE] for i in range(per)], axis=0
        )
        keys = kbuf[:, :, lanes].reshape(n * tok, HEAD_SIZE)
        vals = vbuf[:, :, lanes].reshape(n * tok, HEAD_SIZE)
        scores = lax.dot_general(queries, keys, (((1,), (1,)), ((), ())), preferred_element_type=F32) * scale
        scores = jnp.where(allowed, scores, NEG)
        top = jnp.max(scores, axis=1, keepdims=True)
        probs = jnp.where(allowed, jnp.exp(scores - top), 0.0)
        denom = jnp.sum(probs, axis=1, keepdims=True)
        mixed = jnp.dot(probs.astype(BF16), vals, preferred_element_type=F32)
        done.append((mixed / denom).astype(BF16))
    for d in range(n):
        cut[d] = jnp.concatenate(
            [
                done[g][i * tok : (i + 1) * tok, d * width : (d + 1) * width]
                for g in range(groups)
                for i in range(per)
            ],
            axis=1,
        )
    for k in range(1, n):
        to = peer(z, k, n)
        send(cut.at[to], abuf.at[x, z], a_s.at[k - 1], a_r.at[k - 1], {"seq": to})
    for j in range(1, m):
        send(cut.at[z], abuf.at[x, z], af_s.at[j - 1, 0], af_r.at[j - 1, 0], {"head": peer(x, j, m)})
    abuf[x, z] = cut[z]
    for j in range(1, m):
        s = source(x, j, m)
        arrived(wbuf.at[s, c], w_s.at[j - 1], w_r.at[j - 1], {"head": s})
        for i in range(1, nd):
            send(wbuf.at[s, c], wbuf.at[s, c], wf_s.at[j - 1, i - 1], wf_r.at[j - 1, i - 1], {"dat": peer(c, i, nd)})
    for k in range(1, n):
        s = source(z, k, n)
        arrived(abuf.at[x, s], a_s.at[k - 1], a_r.at[k - 1], {"seq": s})
        for j in range(1, m):
            send(abuf.at[x, s], abuf.at[x, s], af_s.at[j - 1, k], af_r.at[j - 1, k], {"head": peer(x, j, m)})
    for local in local_w:
        local.wait()
    for j in range(1, m):
        s = source(x, j, m)
        for i in range(1, nd):
            d = source(c, i, nd)
            arrived(wbuf.at[s, d], wf_s.at[j - 1, i - 1], wf_r.at[j - 1, i - 1], {"dat": d})
        for k in range(n):
            b = source(z, k, n)
            arrived(abuf.at[s, b], af_s.at[j - 1, k], af_r.at[j - 1, k], {"head": s})

    depth = abuf.shape[3]
    for i in range(nd):
        total = None
        for h in range(m):
            term = jnp.dot(abuf[h].reshape(n * tok, depth), wbuf[h, i], preferred_element_type=F32)
            total = term if total is None else total + term
        part[i] = total.reshape(n, tok, wide).astype(BF16)
        for k in range(1, n):
            to = peer(z, k, n)
            send(part.at[i, to], rbuf.at[k - 1, i], r_s.at[k - 1, i], r_r.at[k - 1, i], {"seq": to})
    for i in range(nd):
        lanes = slice(i * wide, (i + 1) * wide)
        total = part[i, z].astype(F32)
        for k in range(1, n):
            arrived(rbuf.at[k - 1, i], r_s.at[k - 1, i], r_r.at[k - 1, i], {"seq": source(z, k, n)})
            total = total + rbuf[k - 1, i].astype(F32)
        own = (res_ref[:, lanes].astype(F32) + total).astype(BF16)
        own_ref[:, lanes] = own
        st_ref[x, z, i] = own
        mine = st_ref.at[x, z, i]
        for k in range(1, n):
            send(mine, mine, t_s.at[k - 1, i], t_r.at[k - 1, i], {"seq": peer(z, k, n)})
        for j in range(1, m):
            send(mine, mine, tx_s.at[j - 1, 0, i], tx_r.at[j - 1, 0, i], {"head": peer(x, j, m)})
    for i in range(nd):
        for k in range(1, n):
            s = source(z, k, n)
            block = st_ref.at[x, s, i]
            arrived(block, t_s.at[k - 1, i], t_r.at[k - 1, i], {"seq": s})
            for j in range(1, m):
                send(block, block, tx_s.at[j - 1, k, i], tx_r.at[j - 1, k, i], {"head": peer(x, j, m)})
    for k in range(1, n):
        s = source(z, k, n)
        arrived(metas_ref.at[s], me_s.at[k - 1], me_r.at[k - 1], {"seq": s})
    for i in range(nd):
        for j in range(1, m):
            h = source(x, j, m)
            for k in range(n):
                s = source(z, k, n)
                arrived(st_ref.at[h, s, i], tx_s.at[j - 1, k, i], tx_r.at[j - 1, k, i], {"head": h})
    for copy in sends:
        copy.wait_send()


def expert_kernel(n, m, nd, batch, st_ref, metas_ref, gain_ref, wg_ref, wu_ref, out_ref, rows, gates):
    e = pl.program_id(0)
    t = pl.program_id(1)
    experts = rows.shape[0]
    tok, wide = st_ref.shape[3], st_ref.shape[4]
    features = m * nd * wide
    span = batch * tok
    slots = batch * MOST

    @pl.when((e == 0) & (t == 0))
    def _():
        head = lax.axis_index("head")
        r_id = lax.broadcasted_iota(jnp.int32, (span, span), 0)
        c_id = lax.broadcasted_iota(jnp.int32, (span, span), 1)
        before = ((r_id < c_id) & (r_id // tok == c_id // tok)).astype(BF16)
        slot_id = lax.broadcasted_iota(jnp.int32, (slots, span), 0)
        base = (lax.broadcasted_iota(jnp.int32, (1, span), 1) // tok) * MOST
        for b in range(n // batch):
            blocks = slice(b * batch, (b + 1) * batch)
            pieces = [
                st_ref[h, blocks, i].reshape(span, wide).astype(F32) for h in range(m) for i in range(nd)
            ]
            squares = sum(jnp.sum(p * p, axis=1, keepdims=True) for p in pieces)
            factor = lax.rsqrt(squares / features + EPS)
            normed = jnp.concatenate(
                [
                    (p * factor * gain_ref[:, i * wide : (i + 1) * wide].astype(F32)).astype(BF16)
                    for i, p in enumerate(pieces)
                ],
                axis=1,
            )
            meta = jnp.concatenate([metas_ref[b * batch + i] for i in range(batch)], axis=1)
            first, second = meta[0:1], meta[1:2]
            weight = meta[2:3].astype(F32) / 256.0
            for i in range(experts):
                this = head * experts + i
                gate = jnp.where(first == this, weight, 0.0) + jnp.where(second == this, 1.0 - weight, 0.0)
                marked = gate > 0
                spread = jnp.broadcast_to(jnp.where(marked, 1.0, 0.0), (8, span)).astype(BF16)
                rank = jnp.dot(spread, before, preferred_element_type=F32)[0:1].astype(jnp.int32)
                place = jnp.where(marked, rank + base, -1)
                pick = jnp.where(slot_id == place, 1.0, 0.0)
                own = slice(b * slots, (b + 1) * slots)
                rows[i, own] = jnp.dot(pick.astype(BF16), normed, preferred_element_type=F32).astype(BF16)
                gates[i, own] = jnp.sum(pick * gate, axis=1, keepdims=True)

    data = rows[e]
    gate_part = jnp.dot(data, wg_ref[0], preferred_element_type=F32)
    up_part = jnp.dot(data, wu_ref[0], preferred_element_type=F32)
    out_ref[0, 0] = (gates[e] * (gate_part / (1.0 + jnp.exp(-gate_part)) * up_part)).astype(BF16)


def local(
    n, m, nd,
    queries, keys, values, residual_in, out_proj, norm_gain,
    expert_gate, expert_up, routes, gate_numer, sequence_lengths,
):
    tok, feats = queries.shape[1:]
    kv = keys.shape[2]
    share = residual_in.shape[2]
    wide = share // nd
    heads, width, features = out_proj.shape
    depth = heads * width
    experts, _, hidden = expert_gate.shape
    meta = jnp.concatenate([routes[0].T, gate_numer, jnp.zeros((5, tok), jnp.int32)], axis=0)
    vmem = pl.BlockSpec(memory_space=pltpu.VMEM)
    dma = pltpu.SemaphoreType.DMA
    stream_all, own, metas = pl.pallas_call(
        functools.partial(mix_kernel, n, m, nd),
        out_shape=(
            jax.ShapeDtypeStruct((m, n, nd, tok, wide), BF16),
            jax.ShapeDtypeStruct((tok, share), BF16),
            jax.ShapeDtypeStruct((n, 8, tok), jnp.int32),
        ),
        in_specs=[pl.BlockSpec(memory_space=pltpu.SMEM)] + [vmem] * 5 + [pl.BlockSpec(memory_space=pl.ANY)],
        out_specs=(vmem, vmem, vmem),
        scratch_shapes=[
            pltpu.VMEM((n, tok, kv), BF16),
            pltpu.VMEM((n, tok, kv), BF16),
            pltpu.VMEM((m, nd, depth, wide), BF16),
            pltpu.VMEM((n, tok, depth), BF16),
            pltpu.VMEM((m, n, tok, depth), BF16),
            pltpu.VMEM((nd, n, tok, wide), BF16),
            pltpu.VMEM((n - 1, nd, tok, wide), BF16),
            *[dma((n - 1,))] * 6,
            dma((m - 1,)), dma((m - 1,)), dma((m - 1, nd - 1)), dma((m - 1, nd - 1)), dma((nd,)),
            dma((n - 1,)), dma((n - 1,)), dma((m - 1, n)), dma((m - 1, n)),
            dma((n - 1, nd)), dma((n - 1, nd)), dma((n - 1, nd)), dma((n - 1, nd)),
            dma((m - 1, n, nd)), dma((m - 1, n, nd)),
        ],
        compiler_params=pltpu.CompilerParams(
            collective_id=0, has_side_effects=True, vmem_limit_bytes=60 * 1024 * 1024
        ),
    )(
        sequence_lengths, queries[0], keys[0], values[0], meta, residual_in[0],
        out_proj.reshape(depth, features),
    )
    batch = 4 if n % 4 == 0 else n
    tile = min(hidden, 512)
    slots = n * MOST
    weights = pl.BlockSpec((1, features, tile), lambda e, t: (e, 0, t))
    hidden_out = pl.pallas_call(
        functools.partial(expert_kernel, n, m, nd, batch),
        grid=(experts, hidden // tile),
        out_shape=jax.ShapeDtypeStruct((experts, 1, slots, hidden), BF16),
        in_specs=[vmem, vmem, vmem, weights, weights],
        out_specs=pl.BlockSpec((1, 1, slots, tile), lambda e, t: (e, 0, 0, t)),
        scratch_shapes=[pltpu.VMEM((experts, slots, features), BF16), pltpu.VMEM((experts, slots, 1), F32)],
        compiler_params=pltpu.CompilerParams(vmem_limit_bytes=60 * 1024 * 1024),
    )(stream_all, metas, norm_gain[None], expert_gate, expert_up)
    return (own[None], hidden_out)


def solution(mesh):
    seq_spec = P(("grp", "dat"), "seq", "head")
    in_specs = (
        seq_spec, seq_spec, seq_spec, seq_spec,
        P("head", "seq", None), P(),
        P("head", None, "seq"), P("head", None, "seq"),
        P(("grp", "dat"), "seq", None), P(("grp", "dat"), "seq"), P(("grp", "dat")),
    )
    out_specs = (seq_spec, P("head", ("grp", "dat"), None, "seq"))
    body = functools.partial(local, mesh.shape["seq"], mesh.shape["head"], mesh.shape["dat"])
    return jax.shard_map(body, mesh=mesh, in_specs=in_specs, out_specs=out_specs, check_vma=False)
```

```python
import functools
import math

import jax
import jax.numpy as jnp
from jax import lax
from jax.experimental import pallas as pl
from jax.experimental.pallas import tpu as pltpu
from jax.sharding import PartitionSpec as P

HEAD_SIZE = 128
MOST = 40
EPS = 1e-05
NEG = -1e30
RING_BYTES = 40 * 1024 * 1024
MESH = pl.DeviceIdType.MESH
F32 = jnp.float32
BF16 = jnp.bfloat16


def mix_kernel(
    n, m, nd,
    len_ref, q_ref, k_ref, v_ref, route_ref, numer_ref, res_ref, gain_ref, w_ref, wg_ref, wu_ref,
    own_ref, out_ref,
    st_ref, metas_ref, meta_ref, tiles, acc, rows, picks, gates,
    kbuf, vbuf, wbuf, cut, abuf, part, rbuf,
    k_s, k_r, v_s, v_r, me_s, me_r, w_s, w_r, wf_s, wf_r, wl,
    a_s, a_r, af_s, af_r, r_s, r_r, t_s, t_r, tx_s, tx_r, tile_s,
):
    z = lax.axis_index("seq")
    x = lax.axis_index("head")
    c = lax.axis_index("dat")
    tok = q_ref.shape[0]
    heads = q_ref.shape[1] // HEAD_SIZE
    groups = k_ref.shape[1] // HEAD_SIZE
    per = heads // groups
    width = HEAD_SIZE // n
    share = res_ref.shape[1]
    wide = share // nd

    def peer(me, k, size):
        return lax.rem(me + k, size)

    def source(me, k, size):
        return lax.rem(me - k + size, size)

    experts, hidden = acc.shape[0], acc.shape[3]
    step = min(hidden, 512)
    ring = tiles.shape[0]
    order = [(i, e, u, h) for i in range(nd) for e in range(experts) for u in range(2) for h in range(m)]

    def tile_copy(q):
        i, e, u, h = order[q]
        src = (wg_ref, wu_ref)[u].at[e, pl.ds(h * share + i * wide, wide), :]
        return pltpu.make_async_copy(src, tiles.at[q % ring], tile_s.at[q % ring])

    sends = []

    def send(src, dst, s_sem, r_sem, where):
        copy = pltpu.make_async_remote_copy(
            src_ref=src, dst_ref=dst, send_sem=s_sem, recv_sem=r_sem,
            device_id=where, device_id_type=MESH,
        )
        copy.start()
        sends.append(copy)

    def arrived(dst, s_sem, r_sem, where):
        pltpu.make_async_remote_copy(
            src_ref=dst, dst_ref=dst, send_sem=s_sem, recv_sem=r_sem,
            device_id=where, device_id_type=MESH,
        ).wait_recv()

    barrier = pltpu.get_barrier_semaphore()
    for axis, me, size in (("seq", z, n), ("head", x, m), ("dat", c, nd)):
        for k in range(1, size):
            pl.semaphore_signal(barrier, inc=1, device_id={axis: peer(me, k, size)}, device_id_type=MESH)
    local_w = []
    for i in range(nd):
        start = pl.multiple_of(x * share + i * wide, 128)
        local = pltpu.make_async_copy(w_ref.at[:, pl.ds(start, wide)], wbuf.at[x, i], wl.at[i])
        local.start()
        local_w.append(local)
    pl.semaphore_wait(barrier, n - 1 + m - 1 + nd - 1)

    for k in range(1, n):
        to = {"seq": peer(z, k, n)}
        send(k_ref, kbuf.at[z], k_s.at[k - 1], k_r.at[k - 1], to)
        send(v_ref, vbuf.at[z], v_s.at[k - 1], v_r.at[k - 1], to)
    for j in range(1, m):
        to = peer(x, j, m)
        start = pl.multiple_of(to * share + c * wide, 128)
        send(w_ref.at[:, pl.ds(start, wide)], wbuf.at[x, c], w_s.at[j - 1], w_r.at[j - 1], {"head": to})
    for q in range(min(ring, len(order))):
        tile_copy(q).start()
    meta_ref[0:2] = route_ref[...].astype(F32)
    meta_ref[2:3] = numer_ref[...].astype(F32)
    meta_ref[3:8] = jnp.zeros((5, tok), F32)
    for k in range(1, n):
        send(meta_ref, metas_ref.at[z], me_s.at[k - 1], me_r.at[k - 1], {"seq": peer(z, k, n)})
    kbuf[z] = k_ref[...]
    vbuf[z] = v_ref[...]
    metas_ref[z] = meta_ref[...]

    for k in range(1, n):
        s = source(z, k, n)
        arrived(kbuf.at[s], k_s.at[k - 1], k_r.at[k - 1], {"seq": s})
        arrived(vbuf.at[s], v_s.at[k - 1], v_r.at[k - 1], {"seq": s})

    row = lax.broadcasted_iota(jnp.int32, (per * tok, n * tok), 0)
    col = lax.broadcasted_iota(jnp.int32, (per * tok, n * tok), 1)
    allowed = (col <= lax.rem(row, tok) + z * tok) & (col < len_ref[0])
    scale = 1.0 / math.sqrt(HEAD_SIZE)
    done = []
    for g in range(groups):
        lanes = slice(g * HEAD_SIZE, (g + 1) * HEAD_SIZE)
        queries = jnp.concatenate(
            [q_ref[:, (g * per + i) * HEAD_SIZE : (g * per + i + 1) * HEAD_SIZE] for i in range(per)], axis=0
        )
        keys = kbuf[:, :, lanes].reshape(n * tok, HEAD_SIZE)
        vals = vbuf[:, :, lanes].reshape(n * tok, HEAD_SIZE)
        scores = lax.dot_general(queries, keys, (((1,), (1,)), ((), ())), preferred_element_type=F32) * scale
        scores = jnp.where(allowed, scores, NEG)
        top = jnp.max(scores, axis=1, keepdims=True)
        probs = jnp.where(allowed, jnp.exp(scores - top), 0.0)
        denom = jnp.sum(probs, axis=1, keepdims=True)
        mixed = jnp.dot(probs.astype(BF16), vals, preferred_element_type=F32)
        done.append((mixed / denom).astype(BF16))
    for d in range(n):
        cut[d] = jnp.concatenate(
            [
                done[g][i * tok : (i + 1) * tok, d * width : (d + 1) * width]
                for g in range(groups)
                for i in range(per)
            ],
            axis=1,
        )
    for k in range(1, n):
        to = peer(z, k, n)
        send(cut.at[to], abuf.at[x, z], a_s.at[k - 1], a_r.at[k - 1], {"seq": to})
    for j in range(1, m):
        send(cut.at[z], abuf.at[x, z], af_s.at[j - 1, 0], af_r.at[j - 1, 0], {"head": peer(x, j, m)})
    abuf[x, z] = cut[z]
    for j in range(1, m):
        s = source(x, j, m)
        arrived(wbuf.at[s, c], w_s.at[j - 1], w_r.at[j - 1], {"head": s})
        for i in range(1, nd):
            send(wbuf.at[s, c], wbuf.at[s, c], wf_s.at[j - 1, i - 1], wf_r.at[j - 1, i - 1], {"dat": peer(c, i, nd)})
    for k in range(1, n):
        s = source(z, k, n)
        arrived(abuf.at[x, s], a_s.at[k - 1], a_r.at[k - 1], {"seq": s})
        for j in range(1, m):
            send(abuf.at[x, s], abuf.at[x, s], af_s.at[j - 1, k], af_r.at[j - 1, k], {"head": peer(x, j, m)})
    for local in local_w:
        local.wait()
    for j in range(1, m):
        s = source(x, j, m)
        for i in range(1, nd):
            d = source(c, i, nd)
            arrived(wbuf.at[s, d], wf_s.at[j - 1, i - 1], wf_r.at[j - 1, i - 1], {"dat": d})
        for k in range(n):
            b = source(z, k, n)
            arrived(abuf.at[s, b], af_s.at[j - 1, k], af_r.at[j - 1, k], {"head": s})

    depth = abuf.shape[3]
    for i in range(nd):
        total = None
        for h in range(m):
            term = jnp.dot(abuf[h].reshape(n * tok, depth), wbuf[h, i], preferred_element_type=F32)
            total = term if total is None else total + term
        part[i] = total.reshape(n, tok, wide).astype(BF16)
        for k in range(1, n):
            to = peer(z, k, n)
            send(part.at[i, to], rbuf.at[k - 1, i], r_s.at[k - 1, i], r_r.at[k - 1, i], {"seq": to})
    for k in range(1, n):
        s = source(z, k, n)
        arrived(metas_ref.at[s], me_s.at[k - 1], me_r.at[k - 1], {"seq": s})
    batch = 4 if n % 4 == 0 else n
    span = batch * tok
    part_slots = batch * MOST
    r_id = lax.broadcasted_iota(jnp.int32, (span, span), 0)
    c_id = lax.broadcasted_iota(jnp.int32, (span, span), 1)
    before = ((r_id < c_id) & (r_id // tok == c_id // tok)).astype(BF16)
    slot_id = lax.broadcasted_iota(jnp.int32, (part_slots, span), 0)
    base = (lax.broadcasted_iota(jnp.int32, (1, span), 1) // tok) * MOST
    for b in range(n // batch):
        meta = jnp.concatenate([metas_ref[b * batch + i] for i in range(batch)], axis=1)
        weight = meta[2:3] / 256.0
        for e in range(experts):
            this = (x * experts + e).astype(F32)
            gate = jnp.where(meta[0:1] == this, weight, 0.0) + jnp.where(meta[1:2] == this, 1.0 - weight, 0.0)
            marked = gate > 0
            spread = jnp.broadcast_to(jnp.where(marked, 1.0, 0.0), (8, span)).astype(BF16)
            rank = jnp.dot(spread, before, preferred_element_type=F32)[0:1].astype(jnp.int32)
            pick = jnp.where(slot_id == jnp.where(marked, rank + base, -1), 1.0, 0.0)
            picks[e, b] = pick.astype(BF16)
            gates[e, b * part_slots : (b + 1) * part_slots] = jnp.sum(pick * gate, axis=1, keepdims=True)
    for i in range(nd):
        lanes = slice(i * wide, (i + 1) * wide)
        total = part[i, z].astype(F32)
        for k in range(1, n):
            arrived(rbuf.at[k - 1, i], r_s.at[k - 1, i], r_r.at[k - 1, i], {"seq": source(z, k, n)})
            total = total + rbuf[k - 1, i].astype(F32)
        own = (res_ref[:, lanes].astype(F32) + total).astype(BF16)
        own_ref[:, lanes] = own
        st_ref[x, z, i] = own
        mine = st_ref.at[x, z, i]
        for k in range(1, n):
            send(mine, mine, t_s.at[k - 1, i], t_r.at[k - 1, i], {"seq": peer(z, k, n)})
        for j in range(1, m):
            send(mine, mine, tx_s.at[j - 1, 0, i], tx_r.at[j - 1, 0, i], {"head": peer(x, j, m)})
    def pass_on(i, k):
        s = source(z, k, n)
        block = st_ref.at[x, s, i]
        arrived(block, t_s.at[k - 1, i], t_r.at[k - 1, i], {"seq": s})
        for j in range(1, m):
            send(block, block, tx_s.at[j - 1, k, i], tx_r.at[j - 1, k, i], {"head": peer(x, j, m)})

    squares = [jnp.zeros((span, 1), F32) for _ in range(n // batch)]
    for k in range(1, n):
        pass_on(0, k)
    for i in range(nd):
        ahead = [(i + 1, k) for k in range(1, n)] if i + 1 < nd else []
        for j in range(1, m):
            h = source(x, j, m)
            for k in range(n):
                s = source(z, k, n)
                arrived(st_ref.at[h, s, i], tx_s.at[j - 1, k, i], tx_r.at[j - 1, k, i], {"head": h})
        for h in range(m):
            start = h * share + i * wide
            gain = gain_ref[start : start + wide].astype(F32).reshape(1, wide)
            for b in range(n // batch):
                block = st_ref[h, b * batch : (b + 1) * batch, i].reshape(span, wide).astype(F32)
                squares[b] = squares[b] + jnp.sum(block * block, axis=1, keepdims=True)
                scaled = (block * gain).astype(BF16)
                for e in range(experts):
                    rows[e, h, b * part_slots : (b + 1) * part_slots] = jnp.dot(
                        picks[e, b], scaled, preferred_element_type=F32
                    ).astype(BF16)
        for e in range(experts):
            for u in range(2):
                q0 = ((i * experts + e) * 2 + u) * m
                for h in range(m):
                    tile_copy(q0 + h).wait()

                @pl.loop(0, hidden // step)
                def _(t):
                    cols = pl.ds(pl.multiple_of(t * step, step), step)
                    total = None if i == 0 else acc[e, u, :, cols]
                    for h in range(m):
                        term = jnp.dot(rows[e, h], tiles[(q0 + h) % ring, :, cols], preferred_element_type=F32)
                        total = term if total is None else total + term
                    acc[e, u, :, cols] = total

                for h in range(m):
                    if q0 + h + ring < len(order):
                        tile_copy(q0 + h + ring).start()
                if ahead:
                    pass_on(*ahead.pop(0))
        for item in ahead:
            pass_on(*item)
    features = m * share
    for b in range(n // batch):
        factor = jnp.broadcast_to(lax.rsqrt(squares[b] / features + EPS), (span, 128))
        own = slice(b * part_slots, (b + 1) * part_slots)
        for e in range(experts):
            slot_factor = jnp.dot(
                picks[e, b].astype(F32), factor, preferred_element_type=F32, precision=lax.Precision.HIGHEST
            )[:, 0:1]
            slot_gate = gates[e, own]

            @pl.loop(0, hidden // step)
            def _(t):
                cols = pl.ds(pl.multiple_of(t * step, step), step)
                gate_part = acc[e, 0, own, cols] * slot_factor
                up_part = acc[e, 1, own, cols] * slot_factor
                act = gate_part / (1.0 + jnp.exp(-gate_part))
                out_ref[e, 0, own, cols] = (slot_gate * (act * up_part)).astype(BF16)

    for copy in sends:
        copy.wait_send()


def local(
    n, m, nd,
    queries, keys, values, residual_in, out_proj, norm_gain,
    expert_gate, expert_up, routes, gate_numer, sequence_lengths,
):
    tok, feats = queries.shape[1:]
    kv = keys.shape[2]
    share = residual_in.shape[2]
    wide = share // nd
    heads, width, features = out_proj.shape
    depth = heads * width
    experts, _, hidden = expert_gate.shape
    slots = n * MOST
    batch = 4 if n % 4 == 0 else n
    ring = min(2 * m * nd * experts, RING_BYTES // (2 * wide * hidden))
    vmem = pl.BlockSpec(memory_space=pltpu.VMEM)
    hbm = pl.BlockSpec(memory_space=pl.ANY)
    dma = pltpu.SemaphoreType.DMA
    own, hidden_out = pl.pallas_call(
        functools.partial(mix_kernel, n, m, nd),
        out_shape=(
            jax.ShapeDtypeStruct((tok, share), BF16),
            jax.ShapeDtypeStruct((experts, 1, slots, hidden), BF16),
        ),
        in_specs=[pl.BlockSpec(memory_space=pltpu.SMEM)] + [vmem] * 7 + [hbm] * 3,
        out_specs=(vmem, vmem),
        scratch_shapes=[
            pltpu.VMEM((m, n, nd, tok, wide), BF16),
            pltpu.VMEM((n, 8, tok), F32),
            pltpu.VMEM((8, tok), F32),
            pltpu.VMEM((ring, wide, hidden), BF16),
            pltpu.VMEM((experts, 2, slots, hidden), F32),
            pltpu.VMEM((experts, m, slots, wide), BF16),
            pltpu.VMEM((experts, n // batch, batch * MOST, batch * tok), BF16),
            pltpu.VMEM((experts, slots, 1), F32),
            pltpu.VMEM((n, tok, kv), BF16),
            pltpu.VMEM((n, tok, kv), BF16),
            pltpu.VMEM((m, nd, depth, wide), BF16),
            pltpu.VMEM((n, tok, depth), BF16),
            pltpu.VMEM((m, n, tok, depth), BF16),
            pltpu.VMEM((nd, n, tok, wide), BF16),
            pltpu.VMEM((n - 1, nd, tok, wide), BF16),
            *[dma((n - 1,))] * 6,
            dma((m - 1,)), dma((m - 1,)), dma((m - 1, nd - 1)), dma((m - 1, nd - 1)), dma((nd,)),
            dma((n - 1,)), dma((n - 1,)), dma((m - 1, n)), dma((m - 1, n)),
            dma((n - 1, nd)), dma((n - 1, nd)), dma((n - 1, nd)), dma((n - 1, nd)),
            dma((m - 1, n, nd)), dma((m - 1, n, nd)), dma((ring,)),
        ],
        compiler_params=pltpu.CompilerParams(
            collective_id=0, has_side_effects=True, vmem_limit_bytes=63 * 1024 * 1024
        ),
    )(
        sequence_lengths, queries[0], keys[0], values[0], routes[0].T, gate_numer, residual_in[0],
        norm_gain, out_proj.reshape(depth, features), expert_gate, expert_up,
    )
    return (own[None], hidden_out)


def solution(mesh):
    seq_spec = P(("grp", "dat"), "seq", "head")
    in_specs = (
        seq_spec, seq_spec, seq_spec, seq_spec,
        P("head", "seq", None), P(),
        P("head", None, "seq"), P("head", None, "seq"),
        P(("grp", "dat"), "seq", None), P(("grp", "dat"), "seq"), P(("grp", "dat")),
    )
    out_specs = (seq_spec, P("head", ("grp", "dat"), None, "seq"))
    body = functools.partial(local, mesh.shape["seq"], mesh.shape["head"], mesh.shape["dat"])
    return jax.shard_map(body, mesh=mesh, in_specs=in_specs, out_specs=out_specs, check_vma=False)
```

```python
import functools
import math

import jax
import jax.numpy as jnp
from jax import lax
from jax.experimental import pallas as pl
from jax.experimental.pallas import tpu as pltpu
from jax.sharding import PartitionSpec as P

HEAD_SIZE = 128
MOST = 40
EPS = 1e-05
NEG = -1e30
RING_BYTES = 40 * 1024 * 1024
MESH = pl.DeviceIdType.MESH
F32 = jnp.float32
BF16 = jnp.bfloat16


def mix_kernel(
    n, m, nd,
    len_ref, q_ref, k_ref, v_ref, route_ref, numer_ref, res_ref, gain_ref, w_ref, wg_ref, wu_ref,
    own_ref, out_ref,
    st_ref, metas_ref, meta_ref, tiles, acc, rows, picks, gates, factors,
    kbuf, vbuf, wbuf, cut, abuf, part, rbuf,
    k_s, k_r, v_s, v_r, me_s, me_r, w_s, w_r, wf_s, wf_r, wl,
    a_s, a_r, af_s, af_r, r_s, r_r, t_s, t_r, tx_s, tx_r, tile_s,
):
    z = lax.axis_index("seq")
    x = lax.axis_index("head")
    c = lax.axis_index("dat")
    tok = q_ref.shape[0]
    heads = q_ref.shape[1] // HEAD_SIZE
    groups = k_ref.shape[1] // HEAD_SIZE
    per = heads // groups
    width = HEAD_SIZE // n
    share = res_ref.shape[1]
    wide = share // nd

    def peer(me, k, size):
        return lax.rem(me + k, size)

    def source(me, k, size):
        return lax.rem(me - k + size, size)

    experts, hidden = acc.shape[0], acc.shape[3]
    step = min(hidden, 512)
    ring = tiles.shape[0]
    order = [(i, e, u, h) for i in range(nd) for e in range(experts) for u in range(2) for h in range(m)]

    def tile_copy(q):
        i, e, u, h = order[q]
        src = (wg_ref, wu_ref)[u].at[e, pl.ds(h * share + i * wide, wide), :]
        return pltpu.make_async_copy(src, tiles.at[q % ring], tile_s.at[q % ring])

    sends = []

    def send(src, dst, s_sem, r_sem, where):
        copy = pltpu.make_async_remote_copy(
            src_ref=src, dst_ref=dst, send_sem=s_sem, recv_sem=r_sem,
            device_id=where, device_id_type=MESH,
        )
        copy.start()
        sends.append(copy)

    def arrived(dst, s_sem, r_sem, where):
        pltpu.make_async_remote_copy(
            src_ref=dst, dst_ref=dst, send_sem=s_sem, recv_sem=r_sem,
            device_id=where, device_id_type=MESH,
        ).wait_recv()

    barrier = pltpu.get_barrier_semaphore()
    for axis, me, size in (("seq", z, n), ("head", x, m), ("dat", c, nd)):
        for k in range(1, size):
            pl.semaphore_signal(barrier, inc=1, device_id={axis: peer(me, k, size)}, device_id_type=MESH)
    local_w = []
    for i in range(nd):
        start = pl.multiple_of(x * share + i * wide, 128)
        local = pltpu.make_async_copy(w_ref.at[:, pl.ds(start, wide)], wbuf.at[x, i], wl.at[i])
        local.start()
        local_w.append(local)
    pl.semaphore_wait(barrier, n - 1 + m - 1 + nd - 1)

    for k in range(1, n):
        to = {"seq": peer(z, k, n)}
        send(k_ref, kbuf.at[z], k_s.at[k - 1], k_r.at[k - 1], to)
        send(v_ref, vbuf.at[z], v_s.at[k - 1], v_r.at[k - 1], to)
    for j in range(1, m):
        to = peer(x, j, m)
        start = pl.multiple_of(to * share + c * wide, 128)
        send(w_ref.at[:, pl.ds(start, wide)], wbuf.at[x, c], w_s.at[j - 1], w_r.at[j - 1], {"head": to})
    for q in range(min(ring, len(order))):
        tile_copy(q).start()
    meta_ref[0:2] = route_ref[...].astype(F32)
    meta_ref[2:3] = numer_ref[...].astype(F32)
    meta_ref[3:8] = jnp.zeros((5, tok), F32)
    for k in range(1, n):
        send(meta_ref, metas_ref.at[z], me_s.at[k - 1], me_r.at[k - 1], {"seq": peer(z, k, n)})
    kbuf[z] = k_ref[...]
    vbuf[z] = v_ref[...]
    metas_ref[z] = meta_ref[...]

    for k in range(1, n):
        s = source(z, k, n)
        arrived(kbuf.at[s], k_s.at[k - 1], k_r.at[k - 1], {"seq": s})
        arrived(vbuf.at[s], v_s.at[k - 1], v_r.at[k - 1], {"seq": s})

    row = lax.broadcasted_iota(jnp.int32, (per * tok, n * tok), 0)
    col = lax.broadcasted_iota(jnp.int32, (per * tok, n * tok), 1)
    allowed = (col <= lax.rem(row, tok) + z * tok) & (col < len_ref[0])
    scale = 1.0 / math.sqrt(HEAD_SIZE)
    done = []
    for g in range(groups):
        lanes = slice(g * HEAD_SIZE, (g + 1) * HEAD_SIZE)
        queries = jnp.concatenate(
            [q_ref[:, (g * per + i) * HEAD_SIZE : (g * per + i + 1) * HEAD_SIZE] for i in range(per)], axis=0
        )
        keys = kbuf[:, :, lanes].reshape(n * tok, HEAD_SIZE)
        vals = vbuf[:, :, lanes].reshape(n * tok, HEAD_SIZE)
        scores = lax.dot_general(queries, keys, (((1,), (1,)), ((), ())), preferred_element_type=F32) * scale
        scores = jnp.where(allowed, scores, NEG)
        top = jnp.max(scores, axis=1, keepdims=True)
        probs = jnp.where(allowed, jnp.exp(scores - top), 0.0)
        denom = jnp.sum(probs, axis=1, keepdims=True)
        mixed = jnp.dot(probs.astype(BF16), vals, preferred_element_type=F32)
        done.append((mixed / denom).astype(BF16))
    for d in range(n):
        cut[d] = jnp.concatenate(
            [
                done[g][i * tok : (i + 1) * tok, d * width : (d + 1) * width]
                for g in range(groups)
                for i in range(per)
            ],
            axis=1,
        )
    for k in range(1, n):
        to = peer(z, k, n)
        send(cut.at[to], abuf.at[x, z], a_s.at[k - 1], a_r.at[k - 1], {"seq": to})
    for j in range(1, m):
        send(cut.at[z], abuf.at[x, z], af_s.at[j - 1, 0], af_r.at[j - 1, 0], {"head": peer(x, j, m)})
    abuf[x, z] = cut[z]
    for j in range(1, m):
        s = source(x, j, m)
        arrived(wbuf.at[s, c], w_s.at[j - 1], w_r.at[j - 1], {"head": s})
        for i in range(1, nd):
            send(wbuf.at[s, c], wbuf.at[s, c], wf_s.at[j - 1, i - 1], wf_r.at[j - 1, i - 1], {"dat": peer(c, i, nd)})
    for k in range(1, n):
        s = source(z, k, n)
        arrived(abuf.at[x, s], a_s.at[k - 1], a_r.at[k - 1], {"seq": s})
        for j in range(1, m):
            send(abuf.at[x, s], abuf.at[x, s], af_s.at[j - 1, k], af_r.at[j - 1, k], {"head": peer(x, j, m)})
    for local in local_w:
        local.wait()
    for j in range(1, m):
        s = source(x, j, m)
        for i in range(1, nd):
            d = source(c, i, nd)
            arrived(wbuf.at[s, d], wf_s.at[j - 1, i - 1], wf_r.at[j - 1, i - 1], {"dat": d})
        for k in range(n):
            b = source(z, k, n)
            arrived(abuf.at[s, b], af_s.at[j - 1, k], af_r.at[j - 1, k], {"head": s})

    depth = abuf.shape[3]
    for i in range(nd):
        total = None
        for h in range(m):
            term = jnp.dot(abuf[h].reshape(n * tok, depth), wbuf[h, i], preferred_element_type=F32)
            total = term if total is None else total + term
        part[i] = total.reshape(n, tok, wide).astype(BF16)
        for k in range(1, n):
            to = peer(z, k, n)
            send(part.at[i, to], rbuf.at[k - 1, i], r_s.at[k - 1, i], r_r.at[k - 1, i], {"seq": to})
    for k in range(1, n):
        s = source(z, k, n)
        arrived(metas_ref.at[s], me_s.at[k - 1], me_r.at[k - 1], {"seq": s})
    batch = 4 if n % 4 == 0 else n
    span = batch * tok
    part_slots = batch * MOST
    r_id = lax.broadcasted_iota(jnp.int32, (span, span), 0)
    c_id = lax.broadcasted_iota(jnp.int32, (span, span), 1)
    before = ((r_id < c_id) & (r_id // tok == c_id // tok)).astype(BF16)
    slot_id = lax.broadcasted_iota(jnp.int32, (part_slots, span), 0)
    base = (lax.broadcasted_iota(jnp.int32, (1, span), 1) // tok) * MOST
    for b in range(n // batch):
        meta = jnp.concatenate([metas_ref[b * batch + i] for i in range(batch)], axis=1)
        weight = meta[2:3] / 256.0
        for e in range(experts):
            this = (x * experts + e).astype(F32)
            gate = jnp.where(meta[0:1] == this, weight, 0.0) + jnp.where(meta[1:2] == this, 1.0 - weight, 0.0)
            marked = gate > 0
            spread = jnp.broadcast_to(jnp.where(marked, 1.0, 0.0), (8, span)).astype(BF16)
            rank = jnp.dot(spread, before, preferred_element_type=F32)[0:1].astype(jnp.int32)
            pick = jnp.where(slot_id == jnp.where(marked, rank + base, -1), 1.0, 0.0)
            picks[e, b] = pick.astype(BF16)
            gates[e, b * part_slots : (b + 1) * part_slots] = jnp.sum(pick * gate, axis=1, keepdims=True)
    for i in range(nd):
        lanes = slice(i * wide, (i + 1) * wide)
        total = part[i, z].astype(F32)
        for k in range(1, n):
            arrived(rbuf.at[k - 1, i], r_s.at[k - 1, i], r_r.at[k - 1, i], {"seq": source(z, k, n)})
            total = total + rbuf[k - 1, i].astype(F32)
        own = (res_ref[:, lanes].astype(F32) + total).astype(BF16)
        own_ref[:, lanes] = own
        st_ref[x, z, i] = own
        mine = st_ref.at[x, z, i]
        for k in range(1, n):
            send(mine, mine, t_s.at[k - 1, i], t_r.at[k - 1, i], {"seq": peer(z, k, n)})
        for j in range(1, m):
            send(mine, mine, tx_s.at[j - 1, 0, i], tx_r.at[j - 1, 0, i], {"head": peer(x, j, m)})
    def pass_on(i, k):
        s = source(z, k, n)
        block = st_ref.at[x, s, i]
        arrived(block, t_s.at[k - 1, i], t_r.at[k - 1, i], {"seq": s})
        for j in range(1, m):
            send(block, block, tx_s.at[j - 1, k, i], tx_r.at[j - 1, k, i], {"head": peer(x, j, m)})

    squares = [jnp.zeros((span, 1), F32) for _ in range(n // batch)]
    for k in range(1, n):
        pass_on(0, k)
    for i in range(nd):
        ahead = [(i + 1, k) for k in range(1, n)] if i + 1 < nd else []
        for j in range(1, m):
            h = source(x, j, m)
            for k in range(n):
                s = source(z, k, n)
                arrived(st_ref.at[h, s, i], tx_s.at[j - 1, k, i], tx_r.at[j - 1, k, i], {"head": h})
        for h in range(m):
            start = h * share + i * wide
            gain = gain_ref[start : start + wide].astype(F32).reshape(1, wide)
            for b in range(n // batch):
                block = st_ref[h, b * batch : (b + 1) * batch, i].reshape(span, wide).astype(F32)
                squares[b] = squares[b] + jnp.sum(block * block, axis=1, keepdims=True)
                scaled = (block * gain).astype(BF16)
                for e in range(experts):
                    rows[e, h, b * part_slots : (b + 1) * part_slots] = jnp.dot(
                        picks[e, b], scaled, preferred_element_type=F32
                    ).astype(BF16)
        if i == nd - 1:
            for b in range(n // batch):
                factor = jnp.broadcast_to(lax.rsqrt(squares[b] / (m * share) + EPS), (span, 128))
                own = slice(b * part_slots, (b + 1) * part_slots)
                for e in range(experts):
                    factors[e, own] = jnp.dot(
                        picks[e, b].astype(F32), factor, preferred_element_type=F32,
                        precision=lax.Precision.HIGHEST,
                    )[:, 0:1]

        def product(e, u, cols):
            total = None if i == 0 else acc[e, u, :, cols]
            for h in range(m):
                q = ((i * experts + e) * 2 + u) * m + h
                term = jnp.dot(rows[e, h], tiles[q % ring, :, cols], preferred_element_type=F32)
                total = term if total is None else total + term
            return total

        for e in range(experts):
            q0 = (i * experts + e) * 2 * m
            for q in range(q0, q0 + 2 * m):
                tile_copy(q).wait()

            @pl.loop(0, hidden // step)
            def _(t):
                cols = pl.ds(pl.multiple_of(t * step, step), step)
                if i < nd - 1:
                    for u in range(2):
                        acc[e, u, :, cols] = product(e, u, cols)
                else:
                    gate_part = product(e, 0, cols) * factors[e]
                    up_part = product(e, 1, cols) * factors[e]
                    act = gate_part / (1.0 + jnp.exp(-gate_part))
                    out_ref[e, 0, :, cols] = (gates[e] * (act * up_part)).astype(BF16)

            for q in range(q0, q0 + 2 * m):
                if q + ring < len(order):
                    tile_copy(q + ring).start()
            for item in ahead[: -(-(n - 1) // experts)]:
                pass_on(*item)
            ahead = ahead[-(-(n - 1) // experts) :]
        for item in ahead:
            pass_on(*item)
    for copy in sends:
        copy.wait_send()


def place_kernel(own_ref, hidden_ref, own_out, hidden_out, sems):
    first = pltpu.make_async_copy(own_ref, own_out, sems.at[0])
    second = pltpu.make_async_copy(hidden_ref, hidden_out, sems.at[1])
    first.start()
    second.start()
    first.wait()
    second.wait()


def local(
    n, m, nd,
    queries, keys, values, residual_in, out_proj, norm_gain,
    expert_gate, expert_up, routes, gate_numer, sequence_lengths,
):
    tok, feats = queries.shape[1:]
    kv = keys.shape[2]
    share = residual_in.shape[2]
    wide = share // nd
    heads, width, features = out_proj.shape
    depth = heads * width
    experts, _, hidden = expert_gate.shape
    slots = n * MOST
    batch = 4 if n % 4 == 0 else n
    ring = min(2 * m * nd * experts, RING_BYTES // (2 * wide * hidden))
    vmem = pl.BlockSpec(memory_space=pltpu.VMEM)
    hbm = pl.BlockSpec(memory_space=pl.ANY)
    dma = pltpu.SemaphoreType.DMA
    own, hidden_out = pl.pallas_call(
        functools.partial(mix_kernel, n, m, nd),
        out_shape=(
            jax.ShapeDtypeStruct((tok, share), BF16),
            jax.ShapeDtypeStruct((experts, 1, slots, hidden), BF16),
        ),
        in_specs=[pl.BlockSpec(memory_space=pltpu.SMEM)] + [vmem] * 7 + [hbm] * 3,
        out_specs=(vmem, vmem),
        scratch_shapes=[
            pltpu.VMEM((m, n, nd, tok, wide), BF16),
            pltpu.VMEM((n, 8, tok), F32),
            pltpu.VMEM((8, tok), F32),
            pltpu.VMEM((ring, wide, hidden), BF16),
            pltpu.VMEM((experts, 2, slots, hidden), F32),
            pltpu.VMEM((experts, m, slots, wide), BF16),
            pltpu.VMEM((experts, n // batch, batch * MOST, batch * tok), BF16),
            pltpu.VMEM((experts, slots, 1), F32),
            pltpu.VMEM((experts, slots, 1), F32),
            pltpu.VMEM((n, tok, kv), BF16),
            pltpu.VMEM((n, tok, kv), BF16),
            pltpu.VMEM((m, nd, depth, wide), BF16),
            pltpu.VMEM((n, tok, depth), BF16),
            pltpu.VMEM((m, n, tok, depth), BF16),
            pltpu.VMEM((nd, n, tok, wide), BF16),
            pltpu.VMEM((n - 1, nd, tok, wide), BF16),
            *[dma((n - 1,))] * 6,
            dma((m - 1,)), dma((m - 1,)), dma((m - 1, nd - 1)), dma((m - 1, nd - 1)), dma((nd,)),
            dma((n - 1,)), dma((n - 1,)), dma((m - 1, n)), dma((m - 1, n)),
            dma((n - 1, nd)), dma((n - 1, nd)), dma((n - 1, nd)), dma((n - 1, nd)),
            dma((m - 1, n, nd)), dma((m - 1, n, nd)), dma((ring,)),
        ],
        compiler_params=pltpu.CompilerParams(
            collective_id=0, has_side_effects=True, vmem_limit_bytes=63 * 1024 * 1024
        ),
    )(
        sequence_lengths, queries[0], keys[0], values[0], routes[0].T, gate_numer, residual_in[0],
        norm_gain, out_proj.reshape(depth, features), expert_gate, expert_up,
    )
    own, hidden_out = pl.pallas_call(
        place_kernel,
        out_shape=tuple(jax.ShapeDtypeStruct(a.shape, a.dtype) for a in (own, hidden_out)),
        in_specs=[vmem, vmem],
        out_specs=(hbm, hbm),
        scratch_shapes=[dma((2,))],
    )(own, hidden_out)
    return (own[None], hidden_out)


def solution(mesh):
    seq_spec = P(("grp", "dat"), "seq", "head")
    in_specs = (
        seq_spec, seq_spec, seq_spec, seq_spec,
        P("head", "seq", None), P(),
        P("head", None, "seq"), P("head", None, "seq"),
        P(("grp", "dat"), "seq", None), P(("grp", "dat"), "seq"), P(("grp", "dat")),
    )
    out_specs = (seq_spec, P("head", ("grp", "dat"), None, "seq"))
    body = functools.partial(local, mesh.shape["seq"], mesh.shape["head"], mesh.shape["dat"])
    return jax.shard_map(body, mesh=mesh, in_specs=in_specs, out_specs=out_specs, check_vma=False)
```
